32 devices in a mesh: shot: 4 (over y, x), tile: 8 (over z, core).
Axes of the slice: x: 2, y: 2, z: 4, core: 2. Of those that a mesh axis runs over, the one named last changes fastest.
Arguments:
- p_now: float32 [4, 1024, 16, 128], P('shot', 'tile'), may hold values from -6 to 6
- p_prev: float32 [4, 1024, 16, 128], P('shot', 'tile'), may hold values from -6 to 6
- adj_now: float32 [4, 1024, 16, 128], P('shot', 'tile'), may hold values from -60 to 60
- adj_next: float32 [4, 1024, 16, 128], P('shot', 'tile'), may hold values from -60 to 60
- coef_old: float32 [512, 512], P('tile'), may hold values from 0.14 to 0.28
- signs: int32 [4, 512], P('shot', 'tile'), may hold values from 0 to 1
- elem_index: int32 [512], P('tile'), may hold values from 0 to 262143
- wavelet: float32 [5], replicated, may hold values from -4 to 4
Outputs:
- direction: float32 [512, 512], P('tile')
- p_last: float32 [4, 1024, 16, 128], P('shot', 'tile')
The draws below stay inside these ranges and needn't reach their ends.
All inputs are finite; a program needn't handle non-finite values.
Results may differ from the reference program's by a relative error of at most 0.0003.
Values sent between devices are 32-bit elements; how exact they have to be, the bound alone decides.
A program may use at most 64 MiB of HBM per device.

```python
import jax
import jax.numpy as jnp
from jax import lax

CX = 128
CZ = 128
CY = 16
OV = 8
STEPS = 4
ELEM_DEV = 64
CXC = 64
CYC = 8
CZC = 64
NX = 1024
NXC = 512
GROUPS = 4
ELEMS = 512
N_TILE = 8


def adjoint_field(key):
    position = jnp.arange(NX, dtype=jnp.float32) / max(NX - 1, 1)
    shape = (GROUPS, NX, CY, CZ)
    base = jnp.clip(jax.random.normal(key, shape, jnp.float32), -4.0, 4.0)
    scale = jnp.exp(jnp.log(4.0) * position)[:, None, None] * jnp.ones((1, 1, CZ), jnp.float32)
    return base * scale[None]


def draw_adj_now(key, part):
    return adjoint_field(jax.random.fold_in(key, 11))


def draw_adj_next(key, part):
    return adjoint_field(jax.random.fold_in(key, 12))


def plant(values, rng, least, high):
    place = [jax.random.randint(jax.random.fold_in(rng, axis), (), 0, length) for axis, length in enumerate(values.shape)]
    main_axis = values.shape.index(max(values.shape))
    beside = place[:main_axis] + [(place[main_axis] + 1) % values.shape[main_axis]] + place[main_axis + 1:]
    return values.at[tuple(place)].set(least).at[tuple(beside)].set(high)


def shard_levels(key, dims, shards, smallest, largest):
    def one(dim, blocks):
        steps = jax.random.uniform(jax.random.fold_in(jax.random.fold_in(key, 6), dim), (blocks,), jnp.float32, smallest / len(shards), largest / len(shards))
        return jnp.repeat(jnp.exp(steps), dims[dim] // blocks).reshape((-1,) + (1,) * (len(dims) - dim - 1))

    loudness = one(*shards[0])
    for cut in shards[1:]:
        loudness = loudness * one(*cut)
    return loudness


def bell_draw(stream_key, dims, spread, bound, split=(), kind=jnp.bfloat16):
    array = jax.random.normal(stream_key, dims, jnp.float32) * spread
    if len(split) > 0:
        array = shard_levels(stream_key, dims, split, -0.22, 0.18) * array
    return jnp.clip(array, min=-bound, max=bound).astype(kind)


def setup_inputs(seed: int = 0) -> dict:
    key_of = jax.random.split(jax.random.key(seed), 9)
    return {
        "p_now": bell_draw(key_of[0], (GROUPS, NX, CY, CZ), 1.0, 6.0, ((0, 4), (1, 8)), jnp.float32),
        "p_prev": bell_draw(key_of[1], (GROUPS, NX, CY, CZ), 1.0, 6.0, ((0, 4), (1, 8)), jnp.float32),
        "adj_now": draw_adj_now(jax.random.fold_in(key_of[8], 71), 0),
        "adj_next": draw_adj_next(jax.random.fold_in(key_of[8], 71), 0),
        "coef_old": jnp.clip(0.14 + 0.14 * jax.random.uniform(key_of[4], (NXC, CYC * CZC), jnp.float32) ** shard_levels(key_of[4], (NXC, CYC * CZC), ((0, 8),), -0.2, 0.2), 0.14, 0.28),
        "signs": plant(jax.random.randint(key_of[5], (GROUPS, ELEMS), 0, 2), jax.random.fold_in(key_of[5], 1), 0, 1).astype(jnp.int32),
        "elem_index": plant(jax.random.randint(key_of[6], (ELEMS,), 0, CX * CY * CZ), jax.random.fold_in(key_of[6], 1), 0, (CX * CY * CZ) - 1).astype(jnp.int32),
        "wavelet": bell_draw(key_of[7], (STEPS + 1,), 1.0, 4.0, (), jnp.float32),
    }


HIGH = lax.Precision.HIGHEST
LEARN = 0.02
EPSILON = 1e-06

def spectral_second(length):
    index = jnp.arange(length, dtype=jnp.int32)
    phase = index[:, None] * index[None, :] % length
    angle = 2.0 * jnp.pi / length * phase.astype(jnp.float32)
    number = jnp.minimum(index, length - index).astype(jnp.float32) * (2.0 * jnp.pi / length)
    weight = -(number * number) / length
    cosine = jnp.cos(angle)
    sine = jnp.sin(angle)
    first = jnp.dot(cosine * weight[None, :], cosine, precision=HIGH, preferred_element_type=jnp.float32)
    second = jnp.dot(sine * weight[None, :], sine, precision=HIGH, preferred_element_type=jnp.float32)
    return first + second

def taper_bell(inner, margin):
    ramp = jnp.sin(0.5 * jnp.pi * (jnp.arange(margin, dtype=jnp.float32) + 0.5) / margin) ** 2
    return jnp.concatenate([ramp, jnp.ones((inner,), jnp.float32), ramp[::-1]])

def spline_weight(offset):
    mag = jnp.abs(offset)
    inner = 2.0 / 3.0 - mag * mag + 0.5 * mag * mag * mag
    outer = (2.0 - mag) ** 3 / 6.0
    return jnp.where(mag < 1.0, inner, jnp.where(mag < 2.0, outer, 0.0))

def spline_expand_x(fine, coarse):
    rows = jnp.arange(fine, dtype=jnp.int32)[:, None]
    cols = jnp.arange(coarse + 4, dtype=jnp.int32)[None, :] - 2
    return spline_weight(((rows - 2 * cols).astype(jnp.float32) - 0.5) * 0.5)

def spline_project_x(fine, coarse):
    rows = jnp.arange(coarse, dtype=jnp.int32)[:, None]
    cols = jnp.arange(fine + 8, dtype=jnp.int32)[None, :] - 4
    return spline_weight(((cols - 2 * rows).astype(jnp.float32) - 0.5) * 0.5)

def periodic_spline(fine, coarse):
    rows = jnp.arange(fine, dtype=jnp.int32)[:, None]
    cols = jnp.arange(coarse, dtype=jnp.int32)[None, :]
    summed = jnp.zeros((fine, coarse), jnp.float32)
    for image in range(-2, 3):
        summed = summed + spline_weight(((rows - 2 * cols + image * fine).astype(jnp.float32) - 0.5) * 0.5)
    return summed

def laplacian(rimmed, field, second_x, second_z, bell):
    window = rimmed * bell[:, None, None]
    along_x = jnp.einsum('iw,wyz->iyz', second_x, window, precision=HIGH)
    along_z = jnp.einsum('xyz,zk->xyk', field, second_z, precision=HIGH)
    along_y = jnp.roll(field, 1, 1) + jnp.roll(field, -1, 1) - 2.0 * field
    return along_x + along_y + along_z

def expand_local(coef_rim):
    expander = spline_expand_x(CX, CXC)
    wide = jnp.dot(expander, coef_rim, precision=HIGH, preferred_element_type=jnp.float32).reshape(CX, CYC, CZC)
    wide = jnp.einsum('xjk,yj->xyk', wide, periodic_spline(CY, CYC), precision=HIGH)
    return jnp.einsum('xyk,zk->xyz', wide, periodic_spline(CZ, CZC), precision=HIGH)

def project_fine(rimmed):
    projector = spline_project_x(CX, CXC)
    narrow = jnp.dot(projector, rimmed.reshape(CX + 8, CY * CZ), precision=HIGH, preferred_element_type=jnp.float32)
    narrow = narrow.reshape(CXC, CY, CZ)
    narrow = jnp.einsum('xyz,yj->xjz', narrow, periodic_spline(CY, CYC), precision=HIGH)
    narrow = jnp.einsum('xjz,zk->xjk', narrow, periodic_spline(CZ, CZC), precision=HIGH)
    return narrow.reshape(CXC, CYC * CZC)

def reference(p_now, p_prev, adj_now, adj_next, coef_old, signs, elem_index, wavelet):
    second_x = spectral_second(CX + 2 * OV)[OV:OV + CX]
    second_z = spectral_second(CZ)
    bell = taper_bell(CX, OV)
    tiles = jnp.arange(N_TILE, dtype=jnp.int32)
    offsets = (tiles[:, None] * (CX * CY * CZ) + elem_index.reshape(N_TILE, ELEM_DEV)).reshape(-1).astype(jnp.int32)

    def laplace_all(field):
        padded = jnp.pad(field, ((OV, OV), (0, 0), (0, 0)))

        def one_tile(tile):
            rimmed = lax.dynamic_slice_in_dim(padded, tile * CX, CX + 2 * OV, 0)
            core = lax.dynamic_slice_in_dim(field, tile * CX, CX, 0)
            return laplacian(rimmed, core, second_x, second_z, bell)
        return lax.map(one_tile, tiles).reshape(field.shape)

    def expand_all(coef):
        padded = jnp.pad(coef, ((2, 2), (0, 0)))

        def one_tile(tile):
            return expand_local(lax.dynamic_slice_in_dim(padded, tile * CXC, CXC + 4, 0))
        return lax.map(one_tile, tiles).reshape(NX, CY, CZ)

    def project_all(image):
        padded = jnp.pad(image, ((4, 4), (0, 0), (0, 0)))

        def one_tile(tile):
            return project_fine(lax.dynamic_slice_in_dim(padded, tile * CX, CX + 8, 0))
        return lax.map(one_tile, tiles).reshape(NXC, CYC * CZC)

    def inject(field, step, amounts):
        flat = field.reshape(-1).at[offsets].add(wavelet[step] * amounts)
        return flat.reshape(field.shape)
    speed_old = expand_all(coef_old)
    squared_old = speed_old * speed_old

    def one_group(inputs):
        field_now, field_prev, adjoint_now, adjoint_next, sign_row = inputs
        amounts = (2 * sign_row - 1).astype(jnp.float32)
        forward = [field_prev, field_now]
        curvatures = []
        for step in range(STEPS):
            lap_p = laplace_all(forward[-1])
            curvatures.append(lap_p)
            following = 2.0 * forward[-1] - forward[-2] + squared_old * lap_p
            forward.append(inject(following, step, amounts))
        adjoint = [adjoint_next, adjoint_now]
        for step in range(STEPS):
            lap_q = laplace_all(adjoint[-1])
            adjoint.append(2.0 * adjoint[-1] - adjoint[-2] + squared_old * lap_q)
        summed = jnp.zeros_like(field_now)
        for step in range(STEPS):
            summed = summed + adjoint[STEPS + 1 - step] * curvatures[step]
        image = 2.0 * speed_old * summed
        return (project_all(image), forward[-2], forward[-1])
    partials, third, fourth = lax.map(one_group, (p_now, p_prev, adj_now, adj_next, signs))
    total = lax.optimization_barrier(jnp.sum(partials, axis=0))
    scale = jnp.sqrt(jnp.sum(total * total) / (NXC * CYC * CZC) + EPSILON)
    direction = total / scale
    coef_new = coef_old - LEARN * direction
    speed_new = expand_all(coef_new)
    squared_new = speed_new * speed_new

    def last_step(inputs):
        before, latest, sign_row = inputs
        amounts = (2 * sign_row - 1).astype(jnp.float32)
        following = 2.0 * latest - before + squared_new * laplace_all(latest)
        return inject(following, STEPS, amounts)
    p_last = lax.map(last_step, (third, fourth, signs))
    return (direction, p_last)
```

```python
import functools

import jax
import jax.numpy as jnp
import ml_dtypes
import numpy as np
from jax import lax
from jax.experimental import pallas as pl
from jax.experimental.pallas import tpu as pltpu
from jax.sharding import PartitionSpec as P

OV = 8
LEARN = 0.02
EPSILON = 1e-06
F32 = jnp.float32
BF16 = jnp.bfloat16
MESH = pl.DeviceIdType.MESH


def spectral_second(length):
    index = np.arange(length)
    number = np.minimum(index, length - index) * (2.0 * np.pi / length)
    gap = (index[:, None] - index[None, :])[:, :, None] * index[None, None, :] % length
    return np.sum(-(number * number) / length * np.cos(2.0 * np.pi / length * gap), axis=-1)


def spline_weight(offset):
    mag = np.abs(offset)
    inner = 2.0 / 3.0 - mag * mag + 0.5 * mag * mag * mag
    outer = (2.0 - mag) ** 3 / 6.0
    return np.where(mag < 1.0, inner, np.where(mag < 2.0, outer, 0.0))


def periodic_spline(fine, coarse):
    gap = np.arange(fine)[:, None] - 2 * np.arange(coarse)[None, :]
    return sum(spline_weight((gap + image * fine - 0.5) * 0.5) for image in range(-2, 3))


def halves(matrix):
    high = matrix.astype(np.float32).astype(ml_dtypes.bfloat16)
    low = (matrix - high.astype(np.float64)).astype(ml_dtypes.bfloat16)
    return high, low


def twice(block):
    out = np.zeros((2 * block.shape[0], 2 * block.shape[1]))
    out[: block.shape[0], : block.shape[1]] = block
    out[block.shape[0] :, block.shape[1] :] = block
    return out


def constants(cx, cz, cxc, czc):
    full = cx + 2 * OV
    ramp = np.sin(0.5 * np.pi * (np.arange(OV) + 0.5) / OV) ** 2
    second_x = spectral_second(full)[OV : OV + cx]
    high, low = halves(second_x[:, OV : OV + cx])
    core_x = np.block([[high, high], [low, low]])
    rim = np.concatenate([second_x[:, :OV] * ramp, second_x[:, OV + cx :] * ramp[::-1]], 1)
    high, low = halves(rim)
    rim_x = np.block([[high, high], [low, low]])
    high, low = halves(spectral_second(cz))
    core_z = np.block([[high, low], [high, low]])
    gap = np.arange(cx)[:, None] - 2 * (np.arange(cxc + 2 * OV)[None, :] - OV)
    expand_x = spline_weight((gap - 0.5) * 0.5)
    spline_z = periodic_spline(cz, czc)
    floats = [expand_x, twice(spline_z.T), expand_x.T, twice(spline_z)]
    return [core_x, rim_x, core_z] + [m.astype(np.float32) for m in floats]


def split(value):
    high = value.astype(BF16)
    return high, (value - high.astype(F32)).astype(BF16)


def dot(a, b):
    return jnp.dot(a, b, preferred_element_type=F32)


def dot3(a, b):
    ah, al = split(a)
    bh, bl = split(b)
    return dot(ah, bh) + (dot(ah, bl) + dot(al, bh))


def kernel(
    dims, n_shot, n_tile, spline_y,
    p_now, p_prev, q_now, q_next, coef, signs, elems, wave,
    core_x, rim_x, core_z, exp_x, exp_z, pro_x, pro_z,
    direction, p_last,
    raw, raw_sem, pf, qf, lp, lq, sig, sig2, src, wide, exp_t,
    ph, qh, cext, narrow, part0, rims, part, rs, tot, ttot, sq_out, sq_in,
    ph_s, ph_r, qh_s, qh_r, ce_s, ce_r, ri_s, ri_r, rs_s, rs_r, ag_s, ag_r, sq_s, sq_r,
):
    cx, cy, cz, cxc, pairs, steps, group, rows = dims
    shot = lax.axis_index("shot")
    tile = lax.axis_index("tile")
    has_left = tile > 0
    has_right = tile < n_tile - 1
    ext = cxc + 2 * OV

    loads = []
    for i, ref in enumerate((p_now, q_now, p_prev, q_next)):
        copy = pltpu.make_async_copy(ref, raw.at[i], raw_sem.at[i])
        copy.start()
        loads.append(copy)

    barrier = pltpu.get_barrier_semaphore()
    for d in range(1, n_tile):
        pl.semaphore_signal(
            barrier, inc=1, device_id={"tile": lax.rem(tile + d, n_tile)}, device_id_type=MESH
        )
    for d in range(1, n_shot):
        pl.semaphore_signal(
            barrier, inc=1, device_id={"shot": lax.rem(shot + d, n_shot)}, device_id_type=MESH
        )

    def to_planes(i, out):
        loads[i].wait()
        for y in range(cy):
            out[y] = raw[i, pl.ds(y, cx, stride=cy), :]

    for a in range(pairs):
        cext[a, OV : OV + cxc, :] = coef[:, a * 128 : (a + 1) * 128]

    @pl.when(jnp.logical_not(has_left))
    def _():
        ph[:, 0] = jnp.zeros_like(ph[:, 0])
        qh[:, 0] = jnp.zeros_like(qh[:, 0])
        cext[:, :OV, :] = jnp.zeros((pairs, OV, 128), F32)
        rims[0] = jnp.zeros_like(rims[0])

    @pl.when(jnp.logical_not(has_right))
    def _():
        ph[:, 1] = jnp.zeros_like(ph[:, 1])
        qh[:, 1] = jnp.zeros_like(qh[:, 1])
        cext[:, OV + cxc :, :] = jnp.zeros((pairs, OV, 128), F32)
        rims[1] = jnp.zeros_like(rims[1])

    def beside(to_right, right_dst, to_left, left_dst, ss, rr):
        right = pltpu.make_async_remote_copy(
            src_ref=to_right, dst_ref=right_dst, send_sem=ss.at[0], recv_sem=rr.at[0],
            device_id={"tile": lax.rem(tile + 1, n_tile)}, device_id_type=MESH,
        )
        left = pltpu.make_async_remote_copy(
            src_ref=to_left, dst_ref=left_dst, send_sem=ss.at[1], recv_sem=rr.at[1],
            device_id={"tile": lax.rem(tile + n_tile - 1, n_tile)}, device_id_type=MESH,
        )
        return right, left

    def start(pair):
        @pl.when(has_right)
        def _():
            pair[0].start()

        @pl.when(has_left)
        def _():
            pair[1].start()

    def finish(pair):
        @pl.when(has_right)
        def _():
            pair[0].wait_send()
            pair[1].wait_recv()

        @pl.when(has_left)
        def _():
            pair[1].wait_send()
            pair[0].wait_recv()

    def field_halo(field, index, halo, t, ss, rr):
        return beside(
            field.at[index, :, cx - OV :, :], halo.at[t, 0],
            field.at[index, :, :OV, :], halo.at[t, 1], ss.at[t], rr.at[t],
        )

    p_halo = lambda t: field_halo(pf, t + 1, ph, t, ph_s, ph_r)
    q_halo = lambda t: field_halo(qf, t + 1, qh, t, qh_s, qh_r)

    to_planes(0, pf.at[1])
    pl.semaphore_wait(barrier, n_tile + n_shot - 2)
    start(p_halo(0))
    to_planes(1, qf.at[1])
    start(q_halo(0))
    coef_rims = beside(
        cext.at[:, cxc : cxc + OV, :], cext.at[:, :OV, :],
        cext.at[:, OV : 2 * OV, :], cext.at[:, OV + cxc :, :], ce_s, ce_r,
    )
    start(coef_rims)

    def core(field, out):
        def body(i, carry):
            y0 = 2 * i
            y1 = y0 + 1
            a = field[y0]
            b = field[y1]
            high, low = split(jnp.concatenate([a, b], 1))
            ox = dot(core_x[...], jnp.concatenate([high, low], 0))
            oz = dot(
                jnp.concatenate(
                    [
                        jnp.concatenate([high[:, :cz], low[:, :cz]], 1),
                        jnp.concatenate([high[:, cz:], low[:, cz:]], 1),
                    ],
                    0,
                ),
                core_z[...],
            )
            before = field[lax.rem(y0 + cy - 1, cy)]
            after = field[lax.rem(y1 + 1, cy)]
            ox = ox[:cx] + ox[cx:]
            oz = oz[:, :cz] + oz[:, cz:]
            out[y0] = ox[:, :cz] + (before + b - 2.0 * a) + oz[:cx]
            out[y1] = ox[:, cz:] + (a + after - 2.0 * b) + oz[cx:]
            return carry

        lax.fori_loop(0, cy // 2, body, 0, unroll=2)

    def with_rim(halo, lap, use):
        def body(i, carry):
            y0 = 2 * i
            y1 = y0 + 1
            edge = jnp.concatenate(
                [
                    jnp.concatenate([halo[0, y0], halo[0, y1]], 1),
                    jnp.concatenate([halo[1, y0], halo[1, y1]], 1),
                ],
                0,
            )
            ox = dot(rim_x[...], jnp.concatenate(split(edge), 0))
            ox = ox[:cx] + ox[cx:]
            use(y0, lap[y0] + ox[:, :cz])
            use(y1, lap[y1] + ox[:, cz:])
            return carry

        lax.fori_loop(0, cy // 2, body, 0, unroll=2)

    def expand(coefs, out):
        for a in range(pairs):
            both = dot3(dot3(exp_x[...], coefs[a]), exp_z[...])
            wide[2 * a] = both[:, :cz]
            wide[2 * a + 1] = both[:, cz:]

        def body(i, carry):
            at = pl.ds(pl.multiple_of(i * 8, 8), 8)
            planes = [wide[j, at, :] for j in range(2 * pairs)]
            for y in range(cy):
                terms = [
                    float(spline_y[y, j]) * planes[j] for j in range(2 * pairs) if spline_y[y, j] != 0
                ]
                out[y, at, :] = functools.reduce(lambda u, v: u + v, terms)
            return carry

        lax.fori_loop(0, cx // 8, body, 0)

    count = elems.shape[1]
    where_to = elems[...]
    amount = (2 * signs[...] - 1).astype(F32)
    row_of = lax.rem(lax.div(where_to, cz), cy) * cx + lax.div(where_to, cz * cy)
    lanes = (lax.broadcasted_iota(jnp.int32, (cz, count), 0) == lax.rem(where_to, cz)).astype(F32)
    lanes = lanes.astype(BF16)

    def source(y, carry):
        place = lax.broadcasted_iota(jnp.int32, (cx, count), 0) + y * cx
        hits = jnp.where(place == row_of, amount, 0.0).astype(BF16)
        src[y] = lax.dot_general(hits, lanes, (((1,), (1,)), ((), ())), preferred_element_type=F32)
        return carry

    lax.fori_loop(0, cy, source, 0, unroll=2)
    to_planes(2, pf.at[0])
    to_planes(3, qf.at[0])
    finish(coef_rims)
    expand(cext, sig)

    def square(y, carry):
        value = sig[y]
        sig2[y] = value * value
        return carry

    lax.fori_loop(0, cy, square, 0)

    def step(t, carry):
        core(pf.at[t + 1], lp.at[t])
        core(qf.at[t + 1], lq)
        finish(p_halo(t))
        scale = wave[t]

        def use_p(y, lap):
            lp[t, y] = lap
            pf[t + 2, y] = 2.0 * pf[t + 1, y] - pf[t, y] + sig2[y] * lap + scale * src[y]

        with_rim(ph.at[t], lp.at[t], use_p)
        start(p_halo(t + 1))
        finish(q_halo(t))

        def use_q(y, lap):
            qf[t + 2, y] = 2.0 * qf[t + 1, y] - qf[t, y] + sig2[y] * lap

        with_rim(qh.at[t], lq, use_q)

        @pl.when(t < steps - 1)
        def _():
            start(q_halo(t + 1))

        return carry

    lax.fori_loop(0, steps, step, 0)

    def image(i, carry):
        at = pl.ds(pl.multiple_of(i * 8, 8), 8)
        out = [None] * (2 * pairs)
        for y in range(cy):
            summed = qf[steps + 1, y, at, :] * lp[0, y, at, :]
            for t in range(1, steps):
                summed = summed + qf[steps + 1 - t, y, at, :] * lp[t, y, at, :]
            value = 2.0 * sig[y, at, :] * summed
            for j in range(2 * pairs):
                if spline_y[y, j] != 0:
                    term = float(spline_y[y, j]) * value
                    out[j] = term if out[j] is None else out[j] + term
        for j in range(2 * pairs):
            narrow[j, at, :] = out[j]
        return carry

    lax.fori_loop(0, cx // 8, image, 0)
    for a in range(pairs):
        both = jnp.concatenate([narrow[2 * a], narrow[2 * a + 1]], 1)
        part0[a] = dot3(dot3(pro_x[...], both), pro_z[...])
    part_rims = beside(
        part0.at[:, cxc:, :], rims.at[0], part0.at[:, : 2 * OV, :], rims.at[1], ri_s, ri_r
    )
    start(part_rims)
    core(pf.at[steps + 1], lp.at[steps])
    finish(part_rims)
    halfs = ext // rows
    for a in range(pairs):
        whole = jnp.concatenate(
            [
                part0[a, : 2 * OV, :] + rims[0, a],
                part0[a, 2 * OV : cxc, :],
                part0[a, cxc:, :] + rims[1, a],
            ],
            0,
        )
        for r in range(halfs):
            flat = a * halfs + r
            part[flat // group, flat % group] = whole[r * rows : (r + 1) * rows]

    def peer_copy(source_ref, target_ref, d, ss, rr):
        return pltpu.make_async_remote_copy(
            src_ref=source_ref, dst_ref=target_ref, send_sem=ss.at[d - 1], recv_sem=rr.at[d - 1],
            device_id={"shot": lax.rem(shot + d, n_shot)}, device_id_type=MESH,
        )

    scatter = []
    for d in range(1, n_shot):
        copy = peer_copy(part.at[lax.rem(shot + d, n_shot)], rs.at[d - 1], d, rs_s, rs_r)
        copy.start()
        scatter.append(copy)
    finish(p_halo(steps))

    def keep(y, lap):
        lp[steps, y] = lap

    with_rim(ph.at[steps], lp.at[steps], keep)
    mine = part[shot]
    for d in range(1, n_shot):
        scatter[d - 1].wait()
        mine = mine + rs[d - 1]
    tot[shot] = mine
    gather = []
    for d in range(1, n_shot):
        copy = peer_copy(tot.at[shot], tot.at[shot], d, ag_s, ag_r)
        copy.start()
        gather.append(copy)
    for copy in gather:
        copy.wait()
    left_on = jnp.where(has_left, 1.0, 0.0).astype(F32)
    right_on = jnp.where(has_right, 1.0, 0.0).astype(F32)
    squares = jnp.zeros((8, 128), F32)
    for a in range(pairs):
        pieces = []
        for r in range(halfs):
            flat = a * halfs + r
            pieces.append(tot[flat // group, flat % group])
        whole = pieces[0] if halfs == 1 else jnp.concatenate(pieces, 0)
        ttot[a, :OV, :] = whole[:OV] * left_on
        ttot[a, OV : OV + cxc, :] = whole[OV : OV + cxc]
        ttot[a, OV + cxc :, :] = whole[OV + cxc :] * right_on
        for r in range(OV, OV + cxc, 8):
            squares = squares + whole[r : r + 8] * whole[r : r + 8]
    sq_out[...] = squares
    sums = []
    for d in range(1, n_tile):
        copy = pltpu.make_async_remote_copy(
            src_ref=sq_out, dst_ref=sq_in.at[d - 1], send_sem=sq_s.at[d - 1], recv_sem=sq_r.at[d - 1],
            device_id={"tile": lax.rem(tile + d, n_tile)}, device_id_type=MESH,
        )
        copy.start()
        sums.append(copy)
    expand(ttot, exp_t)
    for copy in sums:
        copy.wait()
    for d in range(1, n_tile):
        squares = squares + sq_in[d - 1]
    cells = float(n_tile * cxc * 2 * pairs * 64)
    mean = jnp.sum(jnp.sum(squares, axis=0, keepdims=True), axis=1, keepdims=True) / cells
    scale = 1.0 / jnp.sqrt(mean + EPSILON)
    for a in range(pairs):
        direction[:, a * 128 : (a + 1) * 128] = ttot[a, OV : OV + cxc, :] * scale
    moved = LEARN * scale
    last = wave[steps]
    for y in range(cy):
        speed = sig[y] - moved * exp_t[y]
        p_last[pl.ds(y, cx, stride=cy), :] = (
            2.0 * pf[steps + 1, y] - pf[steps, y] + speed * speed * lp[steps, y] + last * src[y]
        )


def on_device(n_shot, n_tile, p_now, p_prev, adj_now, adj_next, coef_old, signs, elem_index, wavelet):
    _, cx, cy, cz = p_now.shape
    cxc, merged = coef_old.shape
    steps = wavelet.shape[0] - 1
    cyc = cy // 2
    czc = merged // cyc
    pairs = cyc // 2
    spline_y = periodic_spline(cy, cyc).astype(np.float32)
    ext = cxc + 2 * OV
    group = max(1, pairs // n_shot)
    rows = ext // max(1, n_shot // pairs)
    dims = (cx, cy, cz, cxc, pairs, steps, group, rows)
    flat = lambda v: v.reshape(cx * cy, cz)
    consts = [jnp.asarray(c) for c in constants(cx, cz, cxc, czc)]
    vmem = pl.BlockSpec(memory_space=pltpu.VMEM)
    field = (cy, cx, cz)
    buf = lambda *shape: pltpu.VMEM(shape, F32)
    sem = lambda *shape: pltpu.SemaphoreType.DMA(shape)
    direction, p_last = pl.pallas_call(
        functools.partial(kernel, dims, n_shot, n_tile, spline_y),
        out_shape=(
            jax.ShapeDtypeStruct((cxc, merged), F32),
            jax.ShapeDtypeStruct((cx * cy, cz), F32),
        ),
        in_specs=[pl.BlockSpec(memory_space=pl.ANY)] * 4
        + [vmem] * 3
        + [pl.BlockSpec(memory_space=pltpu.SMEM)]
        + [vmem] * len(consts),
        out_specs=(vmem, vmem),
        scratch_shapes=[
            buf(4, cx * cy, cz), sem(4),
            buf(steps + 2, *field), buf(steps + 2, *field), buf(steps + 1, *field), buf(*field),
            buf(*field), buf(*field), buf(*field), buf(cyc, cx, cz), buf(*field),
            buf(steps + 1, 2, cy, OV, cz), buf(steps, 2, cy, OV, cz),
            buf(pairs, ext, 128), buf(cyc, cx, cz), buf(pairs, ext, 128),
            buf(2, pairs, 2 * OV, 128),
            buf(n_shot, group, rows, 128), buf(max(1, n_shot - 1), group, rows, 128),
            buf(n_shot, group, rows, 128), buf(pairs, ext, 128),
            buf(8, 128), buf(max(1, n_tile - 1), 8, 128),
            sem(steps + 1, 2), sem(steps + 1, 2), sem(steps, 2), sem(steps, 2),
            sem(2), sem(2), sem(2), sem(2),
            sem(max(1, n_shot - 1)), sem(max(1, n_shot - 1)),
            sem(max(1, n_shot - 1)), sem(max(1, n_shot - 1)),
            sem(max(1, n_tile - 1)), sem(max(1, n_tile - 1)),
        ],
        compiler_params=pltpu.CompilerParams(
            collective_id=0, has_side_effects=True, vmem_limit_bytes=56 * 1024 * 1024
        ),
    )(
        flat(p_now), flat(p_prev), flat(adj_now), flat(adj_next), coef_old,
        signs, elem_index.reshape(1, -1), wavelet, *consts,
    )
    return direction, p_last.reshape(1, cx, cy, cz)


def solution(mesh):
    placed = (
        P("shot", "tile", None, None),
        P("shot", "tile", None, None),
        P("shot", "tile", None, None),
        P("shot", "tile", None, None),
        P("tile", None),
        P("shot", "tile"),
        P("tile"),
        P(),
    )
    return jax.shard_map(
        functools.partial(on_device, mesh.shape["shot"], mesh.shape["tile"]),
        mesh=mesh,
        in_specs=placed,
        out_specs=(P("tile", None), P("shot", "tile", None, None)),
        check_vma=False,
    )
```

```python
import functools

import jax
import jax.numpy as jnp
import ml_dtypes
import numpy as np
from jax import lax
from jax.experimental import pallas as pl
from jax.experimental.pallas import tpu as pltpu
from jax.sharding import PartitionSpec as P

OV = 8
LEARN = 0.02
EPSILON = 1e-06
F32 = jnp.float32
BF16 = jnp.bfloat16
MESH = pl.DeviceIdType.MESH


def spectral_second(length):
    index = np.arange(length)
    number = np.minimum(index, length - index) * (2.0 * np.pi / length)
    gap = (index[:, None] - index[None, :])[:, :, None] * index[None, None, :] % length
    return np.sum(-(number * number) / length * np.cos(2.0 * np.pi / length * gap), axis=-1)


def spline_weight(offset):
    mag = np.abs(offset)
    inner = 2.0 / 3.0 - mag * mag + 0.5 * mag * mag * mag
    outer = (2.0 - mag) ** 3 / 6.0
    return np.where(mag < 1.0, inner, np.where(mag < 2.0, outer, 0.0))


def periodic_spline(fine, coarse):
    gap = np.arange(fine)[:, None] - 2 * np.arange(coarse)[None, :]
    return sum(spline_weight((gap + image * fine - 0.5) * 0.5) for image in range(-2, 3))


def halves(matrix):
    high = matrix.astype(np.float32).astype(ml_dtypes.bfloat16)
    low = (matrix - high.astype(np.float64)).astype(ml_dtypes.bfloat16)
    return high, low


def twice(block):
    out = np.zeros((2 * block.shape[0], 2 * block.shape[1]))
    out[: block.shape[0], : block.shape[1]] = block
    out[block.shape[0] :, block.shape[1] :] = block
    return out


def constants(cx, cz, cxc, czc):
    full = cx + 2 * OV
    ramp = np.sin(0.5 * np.pi * (np.arange(OV) + 0.5) / OV) ** 2
    second_x = spectral_second(full)[OV : OV + cx]
    high, low = halves(second_x[:, OV : OV + cx])
    core_x = np.block([[high, high], [low, low]])
    rim = np.concatenate([second_x[:, :OV] * ramp, second_x[:, OV + cx :] * ramp[::-1]], 1)
    high, low = halves(rim)
    rim_x = np.block([[high, high], [low, low]])
    high, low = halves(spectral_second(cz))
    core_z = np.block([[high, low], [high, low]])
    gap = np.arange(cx)[:, None] - 2 * (np.arange(cxc + 2 * OV)[None, :] - OV)
    expand_x = spline_weight((gap - 0.5) * 0.5)
    spline_z = periodic_spline(cz, czc)
    floats = [expand_x, twice(spline_z.T), expand_x.T, twice(spline_z)]
    return [core_x, rim_x, core_z] + [m.astype(np.float32) for m in floats]


def split(value):
    high = value.astype(BF16)
    return high, (value - high.astype(F32)).astype(BF16)


def dot(a, b):
    return jnp.dot(a, b, preferred_element_type=F32)


def dot3(a, b):
    ah, al = split(a)
    bh, bl = split(b)
    return dot(ah, bh) + (dot(ah, bl) + dot(al, bh))


def kernel(
    dims, n_shot, n_tile, spline_y,
    p_now, p_prev, q_now, q_next, coef_in, signs, elems, wave,
    core_x_in, rim_x_in, core_z_in, exp_x_in, exp_z_in, pro_x_in, pro_z_in,
    direction, p_last,
    raw, raw_sem, pf, qf, lp, lq, sig, sig2, src, wide, exp_t,
    ph, qh, cext, narrow, part0, rims, part, rs, tot, ttot, sq_out, sq_in,
    ph_s, ph_r, qh_s, qh_r, ce_s, ce_r, ri_s, ri_r, rs_s, rs_r, ag_s, ag_r, sq_s, sq_r,
    sq_all, sa_s, sa_r, consts_sem, coef, core_x, rim_x, core_z, exp_x, exp_z, pro_x, pro_z,
):
    cx, cy, cz, cxc, pairs, steps, group, rows = dims
    shot = lax.axis_index("shot")
    tile = lax.axis_index("tile")
    has_left = tile > 0
    has_right = tile < n_tile - 1
    ext = cxc + 2 * OV

    barrier = pltpu.get_barrier_semaphore()
    for d in range(1, n_tile):
        pl.semaphore_signal(
            barrier, inc=1, device_id={"tile": lax.rem(tile + d, n_tile)}, device_id_type=MESH
        )
    for d in range(1, n_shot):
        pl.semaphore_signal(
            barrier, inc=1, device_id={"shot": lax.rem(shot + d, n_shot)}, device_id_type=MESH
        )

    def load(ref, out, s):
        copy = pltpu.make_async_copy(ref, out, s)
        copy.start()
        return copy

    fields = (p_now, q_now, p_prev, q_next)
    matrices = (
        (core_x_in, core_x), (core_z_in, core_z), (rim_x_in, rim_x), (exp_x_in, exp_x),
        (exp_z_in, exp_z), (pro_x_in, pro_x), (pro_z_in, pro_z),
    )
    loads = [load(fields[0], raw.at[0], raw_sem.at[0])]
    coef_load = load(coef_in, coef, consts_sem.at[0])
    loads.append(load(fields[1], raw.at[1], raw_sem.at[1]))
    matrix_loads = [load(a, b, consts_sem.at[i + 1]) for i, (a, b) in enumerate(matrices)]
    loads += [load(fields[i], raw.at[i], raw_sem.at[i]) for i in (2, 3)]

    def to_planes(i, out):
        loads[i].wait()
        for y in range(cy):
            out[y] = raw[i, pl.ds(y, cx, stride=cy), :]

    @pl.when(jnp.logical_not(has_left))
    def _():
        ph[:, 0] = jnp.zeros_like(ph[:, 0])
        qh[:, 0] = jnp.zeros_like(qh[:, 0])
        cext[:, :OV, :] = jnp.zeros((pairs, OV, 128), F32)
        rims[0] = jnp.zeros_like(rims[0])

    @pl.when(jnp.logical_not(has_right))
    def _():
        ph[:, 1] = jnp.zeros_like(ph[:, 1])
        qh[:, 1] = jnp.zeros_like(qh[:, 1])
        cext[:, OV + cxc :, :] = jnp.zeros((pairs, OV, 128), F32)
        rims[1] = jnp.zeros_like(rims[1])

    def beside(to_right, right_dst, to_left, left_dst, ss, rr):
        right = pltpu.make_async_remote_copy(
            src_ref=to_right, dst_ref=right_dst, send_sem=ss.at[0], recv_sem=rr.at[0],
            device_id={"tile": lax.rem(tile + 1, n_tile)}, device_id_type=MESH,
        )
        left = pltpu.make_async_remote_copy(
            src_ref=to_left, dst_ref=left_dst, send_sem=ss.at[1], recv_sem=rr.at[1],
            device_id={"tile": lax.rem(tile + n_tile - 1, n_tile)}, device_id_type=MESH,
        )
        return right, left

    def start(pair):
        @pl.when(has_right)
        def _():
            pair[0].start()

        @pl.when(has_left)
        def _():
            pair[1].start()

    def finish(pair):
        @pl.when(has_right)
        def _():
            pair[0].wait_send()
            pair[1].wait_recv()

        @pl.when(has_left)
        def _():
            pair[1].wait_send()
            pair[0].wait_recv()

    def field_halo(field, index, halo, t, ss, rr):
        return beside(
            field.at[index, :, cx - OV :, :], halo.at[t, 0],
            field.at[index, :, :OV, :], halo.at[t, 1], ss.at[t], rr.at[t],
        )

    p_halo = lambda t: field_halo(pf, t + 1, ph, t, ph_s, ph_r)
    q_halo = lambda t: field_halo(qf, t + 1, qh, t, qh_s, qh_r)

    to_planes(0, pf.at[1])
    pl.semaphore_wait(barrier, n_tile + n_shot - 2)
    start(p_halo(0))
    to_planes(1, qf.at[1])
    start(q_halo(0))
    coef_load.wait()
    for a in range(pairs):
        cext[a, OV : OV + cxc, :] = coef[:, a * 128 : (a + 1) * 128]
    coef_rims = beside(
        cext.at[:, cxc : cxc + OV, :], cext.at[:, :OV, :],
        cext.at[:, OV : 2 * OV, :], cext.at[:, OV + cxc :, :], ce_s, ce_r,
    )
    start(coef_rims)

    def core(field, out):
        def body(i, carry):
            y0 = 2 * i
            y1 = y0 + 1
            a = field[y0]
            b = field[y1]
            high, low = split(jnp.concatenate([a, b], 1))
            ox = dot(core_x[...], jnp.concatenate([high, low], 0))
            oz = dot(
                jnp.concatenate(
                    [
                        jnp.concatenate([high[:, :cz], low[:, :cz]], 1),
                        jnp.concatenate([high[:, cz:], low[:, cz:]], 1),
                    ],
                    0,
                ),
                core_z[...],
            )
            before = field[lax.rem(y0 + cy - 1, cy)]
            after = field[lax.rem(y1 + 1, cy)]
            ox = ox[:cx] + ox[cx:]
            oz = oz[:, :cz] + oz[:, cz:]
            out[y0] = ox[:, :cz] + (before + b - 2.0 * a) + oz[:cx]
            out[y1] = ox[:, cz:] + (a + after - 2.0 * b) + oz[cx:]
            return carry

        lax.fori_loop(0, cy // 2, body, 0, unroll=2)

    def with_rim(halo, lap, use, out, keep):
        def body(i, carry):
            y0 = 2 * i
            y1 = y0 + 1
            edge = jnp.concatenate(
                [
                    jnp.concatenate([halo[0, y0], halo[0, y1]], 1),
                    jnp.concatenate([halo[1, y0], halo[1, y1]], 1),
                ],
                0,
            )
            ox = dot(rim_x[...], jnp.concatenate(split(edge), 0))
            ox = ox[:cx] + ox[cx:]
            laps = (lap[y0] + ox[:, :cz], lap[y1] + ox[:, cz:])
            nexts = [use(y, value) for y, value in zip((y0, y1), laps)]
            for y, value, new in zip((y0, y1), laps, nexts):
                if keep is not None:
                    keep[y] = value
                if new is not None:
                    out[y] = new
            return carry

        lax.fori_loop(0, cy // 2, body, 0, unroll=2)

    def expand(coefs, out):
        for a in range(pairs):
            both = dot3(dot3(exp_x[...], coefs[a]), exp_z[...])
            wide[2 * a] = both[:, :cz]
            wide[2 * a + 1] = both[:, cz:]

        def body(i, carry):
            at = pl.ds(pl.multiple_of(i * 8, 8), 8)
            planes = [wide[j, at, :] for j in range(2 * pairs)]
            for y in range(cy):
                terms = [
                    float(spline_y[y, j]) * planes[j] for j in range(2 * pairs) if spline_y[y, j] != 0
                ]
                out[y, at, :] = functools.reduce(lambda u, v: u + v, terms)
            return carry

        lax.fori_loop(0, cx // 8, body, 0)

    count = elems.shape[1]
    where_to = elems[...]
    amount = (2 * signs[...] - 1).astype(F32)
    row_of = lax.rem(lax.div(where_to, cz), cy) * cx + lax.div(where_to, cz * cy)
    lanes = (lax.broadcasted_iota(jnp.int32, (cz, count), 0) == lax.rem(where_to, cz)).astype(F32)
    lanes = lanes.astype(BF16)

    def source(y, carry):
        place = lax.broadcasted_iota(jnp.int32, (cx, count), 0) + y * cx
        hits = jnp.where(place == row_of, amount, 0.0).astype(BF16)
        src[y] = lax.dot_general(hits, lanes, (((1,), (1,)), ((), ())), preferred_element_type=F32)
        return carry

    lax.fori_loop(0, cy, source, 0, unroll=2)
    to_planes(2, pf.at[0])
    to_planes(3, qf.at[0])
    for copy in matrix_loads:
        copy.wait()
    finish(coef_rims)
    expand(cext, sig)

    def square(y, carry):
        value = sig[y]
        sig2[y] = value * value
        return carry

    lax.fori_loop(0, cy, square, 0)

    def step(t, carry):
        core(pf.at[t + 1], lp.at[t])
        core(qf.at[t + 1], lq)
        finish(p_halo(t))
        scale = wave[t]

        def use_p(y, lap):
            return 2.0 * pf[t + 1, y] - pf[t, y] + sig2[y] * lap + scale * src[y]

        with_rim(ph.at[t], lp.at[t], use_p, pf.at[t + 2], lp.at[t])
        start(p_halo(t + 1))
        finish(q_halo(t))

        def use_q(y, lap):
            return 2.0 * qf[t + 1, y] - qf[t, y] + sig2[y] * lap

        with_rim(qh.at[t], lq, use_q, qf.at[t + 2], None)

        @pl.when(t < steps - 1)
        def _():
            start(q_halo(t + 1))

        return carry

    lax.fori_loop(0, steps, step, 0)

    def image(i, carry):
        at = pl.ds(pl.multiple_of(i * 8, 8), 8)
        out = [None] * (2 * pairs)
        for y in range(cy):
            summed = qf[steps + 1, y, at, :] * lp[0, y, at, :]
            for t in range(1, steps):
                summed = summed + qf[steps + 1 - t, y, at, :] * lp[t, y, at, :]
            value = 2.0 * sig[y, at, :] * summed
            for j in range(2 * pairs):
                if spline_y[y, j] != 0:
                    term = float(spline_y[y, j]) * value
                    out[j] = term if out[j] is None else out[j] + term
        for j in range(2 * pairs):
            narrow[j, at, :] = out[j]
        return carry

    lax.fori_loop(0, cx // 8, image, 0)
    for a in range(pairs):
        both = jnp.concatenate([narrow[2 * a], narrow[2 * a + 1]], 1)
        part0[a] = dot3(dot3(pro_x[...], both), pro_z[...])
    part_rims = beside(
        part0.at[:, cxc:, :], rims.at[0], part0.at[:, : 2 * OV, :], rims.at[1], ri_s, ri_r
    )
    start(part_rims)
    core(pf.at[steps + 1], lp.at[steps])
    finish(part_rims)
    halfs = ext // rows
    for a in range(pairs):
        whole = jnp.concatenate(
            [
                part0[a, : 2 * OV, :] + rims[0, a],
                part0[a, 2 * OV : cxc, :],
                part0[a, cxc:, :] + rims[1, a],
            ],
            0,
        )
        for r in range(halfs):
            flat = a * halfs + r
            part[flat // group, flat % group] = whole[r * rows : (r + 1) * rows]

    def peer_copy(source_ref, target_ref, d, ss, rr):
        return pltpu.make_async_remote_copy(
            src_ref=source_ref, dst_ref=target_ref, send_sem=ss.at[d - 1], recv_sem=rr.at[d - 1],
            device_id={"shot": lax.rem(shot + d, n_shot)}, device_id_type=MESH,
        )

    scatter = []
    for d in range(1, n_shot):
        copy = peer_copy(part.at[lax.rem(shot + d, n_shot)], rs.at[d - 1], d, rs_s, rs_r)
        copy.start()
        scatter.append(copy)
    finish(p_halo(steps))

    with_rim(ph.at[steps], lp.at[steps], lambda y, lap: None, None, lp.at[steps])
    mine = part[shot]
    for d in range(1, n_shot):
        scatter[d - 1].wait()
        mine = mine + rs[d - 1]
    tot[shot] = mine
    gather = []
    for d in range(1, n_shot):
        copy = peer_copy(tot.at[shot], tot.at[shot], d, ag_s, ag_r)
        copy.start()
        gather.append(copy)
    squares = jnp.zeros((8, 128), F32)
    first = lax.rem(shot, halfs) * rows
    for g in range(group):
        for r in range(0, rows, 8):
            inside = jnp.logical_and(first + r >= OV, first + r < OV + cxc)
            value = mine[g, r : r + 8] * jnp.where(inside, 1.0, 0.0).astype(F32)
            squares = squares + value * mine[g, r : r + 8]
    sq_out[...] = squares
    sums = []
    for d in range(1, n_tile):
        copy = pltpu.make_async_remote_copy(
            src_ref=sq_out, dst_ref=sq_in.at[d - 1], send_sem=sq_s.at[d - 1], recv_sem=sq_r.at[d - 1],
            device_id={"tile": lax.rem(tile + d, n_tile)}, device_id_type=MESH,
        )
        copy.start()
        sums.append(copy)
    for d in range(1, n_tile):
        sums[d - 1].wait()
        squares = squares + sq_in[d - 1]
    sq_all[shot] = squares
    sums = []
    for d in range(1, n_shot):
        copy = peer_copy(sq_all.at[shot], sq_all.at[shot], d, sa_s, sa_r)
        copy.start()
        sums.append(copy)
    for copy in gather:
        copy.wait()
    left_on = jnp.where(has_left, 1.0, 0.0).astype(F32)
    right_on = jnp.where(has_right, 1.0, 0.0).astype(F32)
    for a in range(pairs):
        pieces = []
        for r in range(halfs):
            flat = a * halfs + r
            pieces.append(tot[flat // group, flat % group])
        whole = pieces[0] if halfs == 1 else jnp.concatenate(pieces, 0)
        ttot[a, :OV, :] = whole[:OV] * left_on
        ttot[a, OV : OV + cxc, :] = whole[OV : OV + cxc]
        ttot[a, OV + cxc :, :] = whole[OV + cxc :] * right_on
    expand(ttot, exp_t)
    for copy in sums:
        copy.wait()
    squares = sq_all[0]
    for d in range(1, n_shot):
        squares = squares + sq_all[d]
    cells = float(n_tile * cxc * 2 * pairs * 64)
    mean = jnp.sum(jnp.sum(squares, axis=0, keepdims=True), axis=1, keepdims=True) / cells
    scale = 1.0 / jnp.sqrt(mean + EPSILON)
    for a in range(pairs):
        direction[:, a * 128 : (a + 1) * 128] = ttot[a, OV : OV + cxc, :] * scale
    moved = LEARN * scale
    last = wave[steps]
    for y in range(cy):
        speed = sig[y] - moved * exp_t[y]
        p_last[pl.ds(y, cx, stride=cy), :] = (
            2.0 * pf[steps + 1, y] - pf[steps, y] + speed * speed * lp[steps, y] + last * src[y]
        )


def on_device(n_shot, n_tile, p_now, p_prev, adj_now, adj_next, coef_old, signs, elem_index, wavelet):
    _, cx, cy, cz = p_now.shape
    cxc, merged = coef_old.shape
    steps = wavelet.shape[0] - 1
    cyc = cy // 2
    czc = merged // cyc
    pairs = cyc // 2
    spline_y = periodic_spline(cy, cyc).astype(np.float32)
    ext = cxc + 2 * OV
    group = max(1, pairs // n_shot)
    rows = ext // max(1, n_shot // pairs)
    dims = (cx, cy, cz, cxc, pairs, steps, group, rows)
    flat = lambda v: v.reshape(cx * cy, cz)
    consts = [jnp.asarray(c) for c in constants(cx, cz, cxc, czc)]
    vmem = pl.BlockSpec(memory_space=pltpu.VMEM)
    field = (cy, cx, cz)
    buf = lambda *shape: pltpu.VMEM(shape, F32)
    sem = lambda *shape: pltpu.SemaphoreType.DMA(shape)
    direction, p_last = pl.pallas_call(
        functools.partial(kernel, dims, n_shot, n_tile, spline_y),
        out_shape=(
            jax.ShapeDtypeStruct((cxc, merged), F32),
            jax.ShapeDtypeStruct((cx * cy, cz), F32),
        ),
        in_specs=[pl.BlockSpec(memory_space=pltpu.HBM)] * 5
        + [vmem] * 2
        + [pl.BlockSpec(memory_space=pltpu.SMEM)]
        + [pl.BlockSpec(memory_space=pltpu.HBM)] * len(consts),
        out_specs=(vmem, vmem),
        scratch_shapes=[
            buf(4, cx * cy, cz), sem(4),
            buf(steps + 2, *field), buf(steps + 2, *field), buf(steps + 1, *field), buf(*field),
            buf(*field), buf(*field), buf(*field), buf(cyc, cx, cz), buf(*field),
            buf(steps + 1, 2, cy, OV, cz), buf(steps, 2, cy, OV, cz),
            buf(pairs, ext, 128), buf(cyc, cx, cz), buf(pairs, ext, 128),
            buf(2, pairs, 2 * OV, 128),
            buf(n_shot, group, rows, 128), buf(max(1, n_shot - 1), group, rows, 128),
            buf(n_shot, group, rows, 128), buf(pairs, ext, 128),
            buf(8, 128), buf(max(1, n_tile - 1), 8, 128),
            sem(steps + 1, 2), sem(steps + 1, 2), sem(steps, 2), sem(steps, 2),
            sem(2), sem(2), sem(2), sem(2),
            sem(max(1, n_shot - 1)), sem(max(1, n_shot - 1)),
            sem(max(1, n_shot - 1)), sem(max(1, n_shot - 1)),
            sem(max(1, n_tile - 1)), sem(max(1, n_tile - 1)),
            buf(n_shot, 8, 128), sem(max(1, n_shot - 1)), sem(max(1, n_shot - 1)),
            sem(1 + len(consts)), buf(cxc, merged),
        ]
        + [pltpu.VMEM(c.shape, c.dtype) for c in consts],
        compiler_params=pltpu.CompilerParams(
            collective_id=0, has_side_effects=True, vmem_limit_bytes=38 * 1024 * 1024
        ),
    )(
        flat(p_now), flat(p_prev), flat(adj_now), flat(adj_next), coef_old,
        signs, elem_index.reshape(1, -1), wavelet, *consts,
    )
    return direction, p_last.reshape(1, cx, cy, cz)


def solution(mesh):
    placed = (
        P("shot", "tile", None, None),
        P("shot", "tile", None, None),
        P("shot", "tile", None, None),
        P("shot", "tile", None, None),
        P("tile", None),
        P("shot", "tile"),
        P("tile"),
        P(),
    )
    return jax.shard_map(
        functools.partial(on_device, mesh.shape["shot"], mesh.shape["tile"]),
        mesh=mesh,
        in_specs=placed,
        out_specs=(P("tile", None), P("shot", "tile", None, None)),
        check_vma=False,
    )
```

```python
import functools

import jax
import jax.numpy as jnp
import ml_dtypes
import numpy as np
from jax import lax
from jax.experimental import pallas as pl
from jax.experimental.pallas import tpu as pltpu
from jax.sharding import PartitionSpec as P

OV = 8
LEARN = 0.02
EPSILON = 1e-06
F32 = jnp.float32
BF16 = jnp.bfloat16
MESH = pl.DeviceIdType.MESH


def spectral_second(length):
    index = np.arange(length)
    number = np.minimum(index, length - index) * (2.0 * np.pi / length)
    gap = (index[:, None] - index[None, :])[:, :, None] * index[None, None, :] % length
    return np.sum(-(number * number) / length * np.cos(2.0 * np.pi / length * gap), axis=-1)


def spline_weight(offset):
    mag = np.abs(offset)
    inner = 2.0 / 3.0 - mag * mag + 0.5 * mag * mag * mag
    outer = (2.0 - mag) ** 3 / 6.0
    return np.where(mag < 1.0, inner, np.where(mag < 2.0, outer, 0.0))


def periodic_spline(fine, coarse):
    gap = np.arange(fine)[:, None] - 2 * np.arange(coarse)[None, :]
    return sum(spline_weight((gap + image * fine - 0.5) * 0.5) for image in range(-2, 3))


def halves(matrix):
    high = matrix.astype(np.float32).astype(ml_dtypes.bfloat16)
    low = (matrix - high.astype(np.float64)).astype(ml_dtypes.bfloat16)
    return high, low


def twice(block):
    out = np.zeros((2 * block.shape[0], 2 * block.shape[1]))
    out[: block.shape[0], : block.shape[1]] = block
    out[block.shape[0] :, block.shape[1] :] = block
    return out


def constants(cx, cz, cxc, czc):
    full = cx + 2 * OV
    ramp = np.sin(0.5 * np.pi * (np.arange(OV) + 0.5) / OV) ** 2
    second_x = spectral_second(full)[OV : OV + cx]
    high, low = halves(second_x[:, OV : OV + cx])
    core_x = np.block([[high, high], [low, low]])
    rim = np.concatenate([second_x[:, :OV] * ramp, second_x[:, OV + cx :] * ramp[::-1]], 1)
    high, low = halves(rim)
    rim_x = np.block([[high, high], [low, low]])
    high, low = halves(spectral_second(cz))
    core_z = np.block([[high, low], [high, low]])
    gap = np.arange(cx)[:, None] - 2 * (np.arange(cxc + 2 * OV)[None, :] - OV)
    expand_x = spline_weight((gap - 0.5) * 0.5)
    spline_z = periodic_spline(cz, czc)
    floats = [expand_x, twice(spline_z.T), expand_x.T, twice(spline_z)]
    return [core_x, rim_x, core_z] + [m.astype(np.float32) for m in floats]


def split(value):
    high = value.astype(BF16)
    return high, (value - high.astype(F32)).astype(BF16)


def dot(a, b):
    return jnp.dot(a, b, preferred_element_type=F32)


def dot3(a, b):
    ah, al = split(a)
    bh, bl = split(b)
    return dot(ah, bh) + (dot(ah, bl) + dot(al, bh))


def kernel(
    dims, n_shot, n_tile, spline_y,
    p_now, p_prev, q_now, q_next, coef_in, signs, elems, wave,
    core_x_in, rim_x_in, core_z_in, exp_x_in, exp_z_in, pro_x_in, pro_z_in,
    direction, p_last,
    raw, raw_sem, pf, qf, lp, lq, sig, sig2, src, wide, exp_t,
    ph, qh, cext, narrow, part0, rims, part, rs, tot, ttot, sq_out, sq_in,
    ph_s, ph_r, qh_s, qh_r, ce_s, ce_r, ri_s, ri_r, rs_s, rs_r, ag_s, ag_r, sq_s, sq_r,
    sq_all, sa_s, sa_r, consts_sem, coef, core_x, rim_x, core_z, exp_x, exp_z, pro_x, pro_z,
):
    cx, cy, cz, cxc, pairs, steps, group, rows = dims
    shot = lax.axis_index("shot")
    tile = lax.axis_index("tile")
    has_left = tile > 0
    has_right = tile < n_tile - 1
    ext = cxc + 2 * OV

    barrier = pltpu.get_barrier_semaphore()
    for d in range(1, n_tile):
        pl.semaphore_signal(
            barrier, inc=1, device_id={"tile": lax.rem(tile + d, n_tile)}, device_id_type=MESH
        )
    for d in range(1, n_shot):
        pl.semaphore_signal(
            barrier, inc=1, device_id={"shot": lax.rem(shot + d, n_shot)}, device_id_type=MESH
        )

    def load(ref, out, s):
        copy = pltpu.make_async_copy(ref, out, s)
        copy.start()
        return copy

    fields = (p_now, q_now, p_prev, q_next)
    matrices = (
        (core_x_in, core_x), (core_z_in, core_z), (rim_x_in, rim_x), (exp_x_in, exp_x),
        (exp_z_in, exp_z), (pro_x_in, pro_x), (pro_z_in, pro_z),
    )
    loads = [load(fields[0], raw.at[0], raw_sem.at[0])]
    coef_load = load(coef_in, coef, consts_sem.at[0])
    loads.append(load(fields[1], raw.at[1], raw_sem.at[1]))
    matrix_loads = [load(a, b, consts_sem.at[i + 1]) for i, (a, b) in enumerate(matrices)]
    loads += [load(fields[i], raw.at[i], raw_sem.at[i]) for i in (2, 3)]

    def to_planes(i, out):
        loads[i].wait()
        for y in range(cy):
            out[y] = raw[i, pl.ds(y, cx, stride=cy), :]

    @pl.when(jnp.logical_not(has_left))
    def _():
        ph[:, 0] = jnp.zeros_like(ph[:, 0])
        qh[:, 0] = jnp.zeros_like(qh[:, 0])
        cext[:, :OV, :] = jnp.zeros((pairs, OV, 128), F32)
        rims[0] = jnp.zeros_like(rims[0])

    @pl.when(jnp.logical_not(has_right))
    def _():
        ph[:, 1] = jnp.zeros_like(ph[:, 1])
        qh[:, 1] = jnp.zeros_like(qh[:, 1])
        cext[:, OV + cxc :, :] = jnp.zeros((pairs, OV, 128), F32)
        rims[1] = jnp.zeros_like(rims[1])

    def beside(to_right, right_dst, to_left, left_dst, ss, rr):
        right = pltpu.make_async_remote_copy(
            src_ref=to_right, dst_ref=right_dst, send_sem=ss.at[0], recv_sem=rr.at[0],
            device_id={"tile": lax.rem(tile + 1, n_tile)}, device_id_type=MESH,
        )
        left = pltpu.make_async_remote_copy(
            src_ref=to_left, dst_ref=left_dst, send_sem=ss.at[1], recv_sem=rr.at[1],
            device_id={"tile": lax.rem(tile + n_tile - 1, n_tile)}, device_id_type=MESH,
        )
        return right, left

    def start(pair):
        @pl.when(has_right)
        def _():
            pair[0].start()

        @pl.when(has_left)
        def _():
            pair[1].start()

    def finish(pair):
        @pl.when(has_right)
        def _():
            pair[0].wait_send()
            pair[1].wait_recv()

        @pl.when(has_left)
        def _():
            pair[1].wait_send()
            pair[0].wait_recv()

    def field_halo(field, index, halo, t, ss, rr):
        return beside(
            field.at[index, :, cx - OV :, :], halo.at[t, 0],
            field.at[index, :, :OV, :], halo.at[t, 1], ss.at[t], rr.at[t],
        )

    p_halo = lambda t: field_halo(pf, t + 1, ph, t, ph_s, ph_r)
    q_halo = lambda t: field_halo(qf, t + 1, qh, t, qh_s, qh_r)

    to_planes(0, pf.at[1])
    pl.semaphore_wait(barrier, n_tile + n_shot - 2)
    start(p_halo(0))
    to_planes(1, qf.at[1])
    start(q_halo(0))
    coef_load.wait()
    for a in range(pairs):
        cext[a, OV : OV + cxc, :] = coef[:, a * 128 : (a + 1) * 128]
    coef_rims = beside(
        cext.at[:, cxc : cxc + OV, :], cext.at[:, :OV, :],
        cext.at[:, OV : 2 * OV, :], cext.at[:, OV + cxc :, :], ce_s, ce_r,
    )
    start(coef_rims)

    def core(field, out):
        def body(i, carry):
            y0 = 2 * i
            y1 = y0 + 1
            a = field[y0]
            b = field[y1]
            high, low = split(jnp.concatenate([a, b], 1))
            ox = dot(core_x[...], jnp.concatenate([high, low], 0))
            oz = dot(
                jnp.concatenate(
                    [
                        jnp.concatenate([high[:, :cz], low[:, :cz]], 1),
                        jnp.concatenate([high[:, cz:], low[:, cz:]], 1),
                    ],
                    0,
                ),
                core_z[...],
            )
            before = field[lax.rem(y0 + cy - 1, cy)]
            after = field[lax.rem(y1 + 1, cy)]
            ox = ox[:cx] + ox[cx:]
            oz = oz[:, :cz] + oz[:, cz:]
            out[y0] = ox[:, :cz] + (before + b - 2.0 * a) + oz[:cx]
            out[y1] = ox[:, cz:] + (a + after - 2.0 * b) + oz[cx:]
            return carry

        lax.fori_loop(0, cy // 2, body, 0, unroll=2)

    def with_rim(halo, lap, use, out, keep):
        def body(i, carry):
            y0 = 2 * i
            y1 = y0 + 1
            edge = jnp.concatenate(
                [
                    jnp.concatenate([halo[0, y0], halo[0, y1]], 1),
                    jnp.concatenate([halo[1, y0], halo[1, y1]], 1),
                ],
                0,
            )
            ox = dot(rim_x[...], jnp.concatenate(split(edge), 0))
            ox = ox[:cx] + ox[cx:]
            laps = (lap[y0] + ox[:, :cz], lap[y1] + ox[:, cz:])
            nexts = [use(y, value) for y, value in zip((y0, y1), laps)]
            for y, value, new in zip((y0, y1), laps, nexts):
                if keep is not None:
                    keep[y] = value
                if new is not None:
                    out[y] = new
            return carry

        lax.fori_loop(0, cy // 2, body, 0, unroll=2)

    def expand(coefs, out):
        for a in range(pairs):
            both = dot3(dot3(exp_x[...], coefs[a]), exp_z[...])
            wide[2 * a] = both[:, :cz]
            wide[2 * a + 1] = both[:, cz:]

        def body(i, carry):
            at = pl.ds(pl.multiple_of(i * 8, 8), 8)
            planes = [wide[j, at, :] for j in range(2 * pairs)]
            for y in range(cy):
                terms = [
                    float(spline_y[y, j]) * planes[j] for j in range(2 * pairs) if spline_y[y, j] != 0
                ]
                out[y, at, :] = functools.reduce(lambda u, v: u + v, terms)
            return carry

        lax.fori_loop(0, cx // 8, body, 0)

    count = elems.shape[1]
    where_to = elems[...]
    amount = (2 * signs[...] - 1).astype(F32)
    row_of = lax.rem(lax.div(where_to, cz), cy) * cx + lax.div(where_to, cz * cy)
    lanes = (lax.broadcasted_iota(jnp.int32, (cz, count), 0) == lax.rem(where_to, cz)).astype(F32)
    lanes = lanes.astype(BF16)

    def source(y, carry):
        place = lax.broadcasted_iota(jnp.int32, (cx, count), 0) + y * cx
        hits = jnp.where(place == row_of, amount, 0.0).astype(BF16)
        src[y] = lax.dot_general(hits, lanes, (((1,), (1,)), ((), ())), preferred_element_type=F32)
        return carry

    lax.fori_loop(0, cy, source, 0, unroll=2)
    to_planes(2, pf.at[0])
    to_planes(3, qf.at[0])
    for copy in matrix_loads:
        copy.wait()
    finish(coef_rims)
    expand(cext, sig)

    def square(y, carry):
        value = sig[y]
        sig2[y] = value * value
        return carry

    lax.fori_loop(0, cy, square, 0)

    def step(t, carry):
        core(pf.at[t + 1], lp.at[t])
        core(qf.at[t + 1], lq)
        finish(p_halo(t))
        scale = wave[t]

        def use_p(y, lap):
            return 2.0 * pf[t + 1, y] - pf[t, y] + sig2[y] * lap + scale * src[y]

        with_rim(ph.at[t], lp.at[t], use_p, pf.at[t + 2], lp.at[t])
        start(p_halo(t + 1))
        finish(q_halo(t))

        def use_q(y, lap):
            return 2.0 * qf[t + 1, y] - qf[t, y] + sig2[y] * lap

        with_rim(qh.at[t], lq, use_q, qf.at[t + 2], None)

        @pl.when(t < steps - 1)
        def _():
            start(q_halo(t + 1))

        return carry

    lax.fori_loop(0, steps, step, 0)

    def image(i, carry):
        at = pl.ds(pl.multiple_of(i * 8, 8), 8)
        out = [None] * (2 * pairs)
        for y in range(cy):
            summed = qf[steps + 1, y, at, :] * lp[0, y, at, :]
            for t in range(1, steps):
                summed = summed + qf[steps + 1 - t, y, at, :] * lp[t, y, at, :]
            value = 2.0 * sig[y, at, :] * summed
            for j in range(2 * pairs):
                if spline_y[y, j] != 0:
                    term = float(spline_y[y, j]) * value
                    out[j] = term if out[j] is None else out[j] + term
        for j in range(2 * pairs):
            narrow[j, at, :] = out[j]
        return carry

    lax.fori_loop(0, cx // 8, image, 0)
    for a in range(pairs):
        both = jnp.concatenate([narrow[2 * a], narrow[2 * a + 1]], 1)
        part0[a] = dot3(dot3(pro_x[...], both), pro_z[...])
    part_rims = beside(
        part0.at[:, cxc:, :], rims.at[0], part0.at[:, : 2 * OV, :], rims.at[1], ri_s, ri_r
    )
    start(part_rims)
    core(pf.at[steps + 1], lp.at[steps])
    finish(part_rims)
    halfs = ext // rows
    for a in range(pairs):
        whole = jnp.concatenate(
            [
                part0[a, : 2 * OV, :] + rims[0, a],
                part0[a, 2 * OV : cxc, :],
                part0[a, cxc:, :] + rims[1, a],
            ],
            0,
        )
        for r in range(halfs):
            flat = a * halfs + r
            part[flat // group, flat % group] = whole[r * rows : (r + 1) * rows]

    def peer_copy(source_ref, target_ref, d, ss, rr):
        return pltpu.make_async_remote_copy(
            src_ref=source_ref, dst_ref=target_ref, send_sem=ss.at[d - 1], recv_sem=rr.at[d - 1],
            device_id={"shot": lax.rem(shot + d, n_shot)}, device_id_type=MESH,
        )

    scatter = []
    for d in range(1, n_shot):
        copy = peer_copy(part.at[lax.rem(shot + d, n_shot)], rs.at[d - 1], d, rs_s, rs_r)
        copy.start()
        scatter.append(copy)
    finish(p_halo(steps))

    with_rim(ph.at[steps], lp.at[steps], lambda y, lap: None, None, lp.at[steps])
    mine = part[shot]
    for d in range(1, n_shot):
        scatter[d - 1].wait()
        mine = mine + rs[d - 1]
    tot[shot] = mine
    gather = []
    for d in range(1, n_shot):
        copy = peer_copy(tot.at[shot], tot.at[shot], d, ag_s, ag_r)
        copy.start()
        gather.append(copy)
    squares = jnp.zeros((8, 128), F32)
    first = lax.rem(shot, halfs) * rows
    for g in range(group):
        for r in range(0, rows, 8):
            inside = jnp.logical_and(first + r >= OV, first + r < OV + cxc)
            value = mine[g, r : r + 8] * jnp.where(inside, 1.0, 0.0).astype(F32)
            squares = squares + value * mine[g, r : r + 8]
    sq_out[...] = squares
    sums = []
    for d in range(1, n_tile):
        copy = pltpu.make_async_remote_copy(
            src_ref=sq_out, dst_ref=sq_in.at[d - 1], send_sem=sq_s.at[d - 1], recv_sem=sq_r.at[d - 1],
            device_id={"tile": lax.rem(tile + d, n_tile)}, device_id_type=MESH,
        )
        copy.start()
        sums.append(copy)
    for d in range(1, n_tile):
        sums[d - 1].wait()
        squares = squares + sq_in[d - 1]
    sq_all[shot] = squares
    sums = []
    for d in range(1, n_shot):
        copy = peer_copy(sq_all.at[shot], sq_all.at[shot], d, sa_s, sa_r)
        copy.start()
        sums.append(copy)
    for copy in gather:
        copy.wait()
    left_on = jnp.where(has_left, 1.0, 0.0).astype(F32)
    right_on = jnp.where(has_right, 1.0, 0.0).astype(F32)
    for a in range(pairs):
        pieces = []
        for r in range(halfs):
            flat = a * halfs + r
            pieces.append(tot[flat // group, flat % group])
        whole = pieces[0] if halfs == 1 else jnp.concatenate(pieces, 0)
        ttot[a, :OV, :] = whole[:OV] * left_on
        ttot[a, OV : OV + cxc, :] = whole[OV : OV + cxc]
        ttot[a, OV + cxc :, :] = whole[OV + cxc :] * right_on
    expand(ttot, exp_t)
    for copy in sums:
        copy.wait()
    squares = sq_all[0]
    for d in range(1, n_shot):
        squares = squares + sq_all[d]
    cells = float(n_tile * cxc * 2 * pairs * 64)
    mean = jnp.sum(jnp.sum(squares, axis=0, keepdims=True), axis=1, keepdims=True) / cells
    scale = 1.0 / jnp.sqrt(mean + EPSILON)
    for a in range(pairs):
        direction[:, a * 128 : (a + 1) * 128] = ttot[a, OV : OV + cxc, :] * scale
    moved = LEARN * scale
    last = wave[steps]
    for y in range(cy):
        speed = sig[y] - moved * exp_t[y]
        p_last[pl.ds(y, cx, stride=cy), :] = (
            2.0 * pf[steps + 1, y] - pf[steps, y] + speed * speed * lp[steps, y] + last * src[y]
        )


def on_device(n_shot, n_tile, p_now, p_prev, adj_now, adj_next, coef_old, signs, elem_index, wavelet):
    _, cx, cy, cz = p_now.shape
    cxc, merged = coef_old.shape
    steps = wavelet.shape[0] - 1
    cyc = cy // 2
    czc = merged // cyc
    pairs = cyc // 2
    spline_y = periodic_spline(cy, cyc).astype(np.float32)
    ext = cxc + 2 * OV
    group = max(1, pairs // n_shot)
    rows = ext // max(1, n_shot // pairs)
    dims = (cx, cy, cz, cxc, pairs, steps, group, rows)
    flat = lambda v: v.reshape(cx * cy, cz)
    consts = [jnp.asarray(c) for c in constants(cx, cz, cxc, czc)]
    vmem = pl.BlockSpec(memory_space=pltpu.VMEM)
    held = lambda v: pltpu.with_memory_space_constraint(v, pltpu.HBM)
    field = (cy, cx, cz)
    buf = lambda *shape: pltpu.VMEM(shape, F32)
    sem = lambda *shape: pltpu.SemaphoreType.DMA(shape)
    direction, p_last = pl.pallas_call(
        functools.partial(kernel, dims, n_shot, n_tile, spline_y),
        out_shape=(
            jax.ShapeDtypeStruct((cxc, merged), F32),
            jax.ShapeDtypeStruct((cx * cy, cz), F32),
        ),
        in_specs=[pl.BlockSpec(memory_space=pltpu.HBM)] * 5
        + [vmem] * 2
        + [pl.BlockSpec(memory_space=pltpu.SMEM)]
        + [pl.BlockSpec(memory_space=pltpu.HBM)] * len(consts),
        out_specs=(vmem, vmem),
        scratch_shapes=[
            buf(4, cx * cy, cz), sem(4),
            buf(steps + 2, *field), buf(steps + 2, *field), buf(steps + 1, *field), buf(*field),
            buf(*field), buf(*field), buf(*field), buf(cyc, cx, cz), buf(*field),
            buf(steps + 1, 2, cy, OV, cz), buf(steps, 2, cy, OV, cz),
            buf(pairs, ext, 128), buf(cyc, cx, cz), buf(pairs, ext, 128),
            buf(2, pairs, 2 * OV, 128),
            buf(n_shot, group, rows, 128), buf(max(1, n_shot - 1), group, rows, 128),
            buf(n_shot, group, rows, 128), buf(pairs, ext, 128),
            buf(8, 128), buf(max(1, n_tile - 1), 8, 128),
            sem(steps + 1, 2), sem(steps + 1, 2), sem(steps, 2), sem(steps, 2),
            sem(2), sem(2), sem(2), sem(2),
            sem(max(1, n_shot - 1)), sem(max(1, n_shot - 1)),
            sem(max(1, n_shot - 1)), sem(max(1, n_shot - 1)),
            sem(max(1, n_tile - 1)), sem(max(1, n_tile - 1)),
            buf(n_shot, 8, 128), sem(max(1, n_shot - 1)), sem(max(1, n_shot - 1)),
            sem(1 + len(consts)), buf(cxc, merged),
        ]
        + [pltpu.VMEM(c.shape, c.dtype) for c in consts],
        compiler_params=pltpu.CompilerParams(
            collective_id=0, has_side_effects=True, vmem_limit_bytes=38 * 1024 * 1024
        ),
    )(
        *map(held, (flat(p_now), flat(p_prev), flat(adj_now), flat(adj_next), coef_old)),
        signs, elem_index.reshape(1, -1), wavelet, *map(held, consts),
    )
    return direction, p_last.reshape(1, cx, cy, cz)


def solution(mesh):
    placed = (
        P("shot", "tile", None, None),
        P("shot", "tile", None, None),
        P("shot", "tile", None, None),
        P("shot", "tile", None, None),
        P("tile", None),
        P("shot", "tile"),
        P("tile"),
        P(),
    )
    return jax.shard_map(
        functools.partial(on_device, mesh.shape["shot"], mesh.shape["tile"]),
        mesh=mesh,
        in_specs=placed,
        out_specs=(P("tile", None), P("shot", "tile", None, None)),
        check_vma=False,
    )
```
